128 devices in a mesh: row: 8 (over y, core), col: 16 (over z, x).
Axes of the slice: x: 4, y: 4, z: 4, core: 2. Of those that a mesh axis runs over, the one named last changes fastest.
Arguments:
- pan_left: bfloat16 [32, 2048, 512], P('row', 'col'), may hold values from -6 to 6
- pan_right: bfloat16 [32, 2048, 512], P('row', 'col'), may hold values from -0.125 to 0.125
- inverse: bfloat16 [2048, 2048], P('col'), may hold values from -0.25 to 1.25, as said below
- rank_list: int32 [32], replicated, may hold values from 32 to 512, as said below
Outputs:
- update_right: bfloat16 [32, 32, 2048, 512], P('row', 'col')
- update_gram: bfloat16 [32, 32, 512, 512], P('row', 'col')
The draws below stay inside these ranges and needn't reach their ends.
Inputs may be any that keep to these rules, and one draw needn't show every extreme that they name: `inverse`: lower triangular; diagonal entries lie from 0.75 to 1.25. `rank_list`: columns of a tile's factors at or beyond its rank do not count.
All inputs are finite; a program needn't handle non-finite values.
Results may differ from the reference program's by a relative error of at most 0.0065.
Values may be sent and summed in bfloat16 or wider, within the bound.
A program may use at most 128 MiB of HBM per device.

```python
import math
import jax
import jax.numpy as jnp
from jax import lax

NB = 2048
RMAX = 512
NP = 32


def draw_inverse(key, part):
    base = jax.random.fold_in(key, 17)
    first, second = jax.random.split(base)
    spread = jnp.clip(jax.random.normal(first, (NB, NB), jnp.float32), -4.0, 4.0)
    lower = jnp.tril(spread * (0.5 / math.sqrt(NB)), -1)
    diag_part = 0.75 + 0.5 * jax.random.uniform(second, (NB,), jnp.float32)
    return (lower + jnp.diag(diag_part)).astype(jnp.bfloat16)


def draw_rank_list(key, part):
    base = jax.random.fold_in(key, 29)
    first, second, third = jax.random.split(base, 3)
    lowest = RMAX // 16
    values = jax.random.randint(first, (NP,), lowest, RMAX + 1, dtype=jnp.int32)
    high_spot = jax.random.randint(second, (), 0, NP, dtype=jnp.int32)
    offset = jax.random.randint(third, (), 1, NP, dtype=jnp.int32)
    low_spot = (high_spot + offset) % NP
    values = values.at[high_spot].set(RMAX).at[low_spot].set(lowest)
    return values


def block_scale(rng, shape, cuts, smallest, high):
    loudness = 1.0
    for position, blocks in cuts:
        steps = jax.random.uniform(jax.random.fold_in(jax.random.fold_in(rng, 6), position), (blocks,), jnp.float32, smallest / len(cuts), high / len(cuts))
        loudness = loudness * jnp.repeat(jnp.exp(steps), shape[position] // blocks).reshape((-1,) + (1,) * (len(shape) - 1 - position))
    return loudness


def noise(stream_key, dims, width, most, cuts=(), kind=jnp.bfloat16):
    drawn = jax.random.normal(stream_key, dims, jnp.float32) * width
    if len(cuts) > 0:
        drawn = block_scale(stream_key, dims, cuts, -0.22, 0.18) * drawn
    return jnp.clip(drawn, min=-most, max=most).astype(kind)


def setup_inputs(seed: int = 0) -> dict:
    seeds = jax.random.split(jax.random.key(seed), 5)
    pan_left = noise(seeds[0], (NP, NB, RMAX), 1.0, 6.0, ((0, 8), (1, 16)))
    pan_right = noise(seeds[1], (NP, NB, RMAX), NB ** -0.5, 0.125, ((0, 8), (1, 16)))
    inverse = draw_inverse(jax.random.fold_in(seeds[4], 71), 0)
    rank_list = draw_rank_list(jax.random.fold_in(seeds[4], 71), 0)
    return dict(pan_left=pan_left, pan_right=pan_right, inverse=inverse, rank_list=rank_list)


def solve_tile(factor, inverse):
    return jnp.dot(inverse, factor, preferred_element_type=jnp.float32).astype(jnp.bfloat16)


def reference(pan_left, pan_right, inverse, rank_list):
    solved = lax.map(lambda factor: solve_tile(factor, inverse), pan_right)
    live = (jnp.arange(RMAX, dtype=jnp.int32)[None, :] < rank_list[:, None]).astype(jnp.float32)
    indices = jnp.arange(NP, dtype=jnp.int32)

    def one_pair(first, second):
        core = lax.dot_general(solved[first], solved[second], (((0,), (0,)), ((), ())), preferred_element_type=jnp.float32)
        core = (core * live[first][:, None] * live[second][None, :]).astype(jnp.bfloat16)
        update = lax.dot_general(pan_left[second], core, (((1,), (1,)), ((), ())), preferred_element_type=jnp.float32).astype(jnp.bfloat16)
        gram = (lax.dot_general(update, update, (((0,), (0,)), ((), ())), preferred_element_type=jnp.float32) / NB).astype(jnp.bfloat16)
        return update, gram

    def one_row(first):
        return lax.map(lambda second: one_pair(first, second), indices)

    update, gram = lax.map(one_row, indices)
    return update, gram
```

```python
import functools

import jax
import jax.numpy as jnp
from jax import lax
from jax.experimental import pallas as pl
from jax.experimental.pallas import tpu as pltpu
from jax.sharding import PartitionSpec as P

MESH = pl.DeviceIdType.MESH
BF = jnp.bfloat16
F32 = jnp.float32


def device(x, y, z, p):
    return (lax.rem(y, 4) * 2 + p, lax.rem(z, 4) * 4 + lax.rem(x, 4))


def run_if(condition, body):
    if condition is None:
        body()
    else:
        pl.when(condition)(body)


class Semaphores:
    def __init__(self, send, recv):
        self.send, self.recv, self.used = send, recv, 0

    def take(self, count):
        first = self.used
        self.used += count
        return first

    def copy(self, src, dst, send, recv, target):
        return pltpu.make_async_remote_copy(
            src_ref=src, dst_ref=dst, send_sem=self.send.at[send], recv_sem=self.recv.at[recv],
            device_id=target, device_id_type=MESH,
        )


class Ring:
    def __init__(self, sems, me, plus, minus, view, half, has=lambda slot: None):
        self.sems, self.plus, self.minus = sems, plus, minus
        self.view, self.half, self.has = view, half, has
        self.me, self.left, self.right, self.far = me, lax.rem(me + 3, 4), lax.rem(me + 1, 4), lax.rem(me + 2, 4)
        self.base = sems.take(4)

    def message(self, ref, which, target):
        return self.sems.copy(ref, ref, self.base + which, self.base + which, target)

    def start(self):
        def go():
            self.message(self.view(self.me), 0, self.plus).start()
            self.message(self.view(self.me), 1, self.minus).start()

        run_if(self.has(self.me), go)

    def forward(self):
        def from_left():
            self.message(self.view(self.left), 0, self.plus).wait_recv()
            self.message(self.half(self.left, 0), 2, self.plus).start()

        def from_right():
            self.message(self.view(self.right), 1, self.minus).wait_recv()
            self.message(self.half(self.right, 1), 3, self.minus).start()

        run_if(self.has(self.left), from_left)
        run_if(self.has(self.right), from_right)

    def finish(self):
        def go():
            self.message(self.half(self.far, 0), 2, self.plus).wait_recv()
            self.message(self.half(self.far, 1), 3, self.minus).wait_recv()

        run_if(self.has(self.far), go)

    def drain(self):
        def own():
            self.message(self.view(self.me), 0, self.plus).wait_send()
            self.message(self.view(self.me), 1, self.minus).wait_send()

        run_if(self.has(self.me), own)
        run_if(self.has(self.left), lambda: self.message(self.half(self.left, 0), 2, self.plus).wait_send())
        run_if(self.has(self.right), lambda: self.message(self.half(self.right, 1), 3, self.minus).wait_send())


def dot_tn(a, b):
    return lax.dot_general(a, b, (((0,), (0,)), ((), ())), preferred_element_type=F32)


def gather_kernel(
    left_ref, right_ref, inv_ref, rank_ref, core_out, left_out,
    rbuf, abuf, wbuf, lbuf, rjp, sjp, cores, send_sem, recv_sem, local_sem,
):
    row, col = lax.axis_index("row"), lax.axis_index("col")
    x, z, y, p = lax.rem(col, 4), lax.div(col, 4), lax.div(row, 2), lax.rem(row, 2)
    xp, xm = device(x + 1, y, z, p), device(x + 3, y, z, p)
    yp, ym = device(x, y + 1, z, p), device(x, y + 3, z, p)
    zp, zm = device(x, y, z + 1, p), device(x, y, z + 3, p)
    mate = device(x, y, z, 1 - p)
    sems = Semaphores(send_sem, recv_sem)

    own_right = pltpu.make_async_copy(right_ref, rbuf.at[:, z, x], local_sem.at[0])
    own_right.start()
    own_inv = [pltpu.make_async_copy(inv_ref.at[p, :, :, 512 * k:512 * k + 512], abuf.at[k, z, x, p], local_sem.at[1 + k]) for k in range(4)]
    for k in range(4):
        own_inv[k].start()

    barrier = pltpu.get_barrier_semaphore()
    for target in (xp, xm, yp, ym, zp, zm, mate):
        pl.semaphore_signal(barrier, inc=1, device_id=target, device_id_type=MESH)
    for source in range(16):
        pl.semaphore_signal(barrier, inc=1, device_id=device(source % 4, z, source // 4, lax.div(x, 2)), device_id_type=MESH)
    pl.semaphore_wait(barrier, 23)

    pieces = sems.take(32)
    at_home = jnp.logical_and(y == z, p == lax.div(x, 2))

    def piece(which, m):
        edge, y_to, p_to = m // 8, (m // 2) % 4, m % 2
        x_to = 2 * p + edge
        columns = slice(128 * y_to, 128 * y_to + 128)
        mine = jnp.logical_and(jnp.logical_and(at_home, x_to == x), jnp.logical_and(y_to == y, p_to == p))
        if which == 0:
            src, dst = right_ref.at[2 * edge + p_to, :, :, columns], rjp.at[col]
        else:
            src, dst = left_ref.at[2 * edge + p_to, :, :, columns], lbuf.at[p_to, col, :, :, columns]
        remote = sems.copy(src, dst, pieces + 16 * which + m, pieces + 16 * which + col, device(x_to, y_to, y, p_to))
        return mine, pltpu.make_async_copy(src, dst, local_sem.at[5 + which]), remote

    def send_pieces(which):
        for m in range(16):
            mine, local, remote = piece(which, m)
            pl.when(mine)(local.start)
            pl.when(jnp.logical_not(mine))(remote.start)

    def take_pieces(which):
        ycol = pl.ds(pl.multiple_of(128 * y, 128), 128)
        for source in range(16):
            dst = rjp.at[source] if which == 0 else lbuf.at[p, source, :, :, ycol]
            mine = jnp.logical_and(at_home, col == source)
            pl.when(mine)(pltpu.make_async_copy(dst, dst, local_sem.at[5 + which]).wait)
            pl.when(jnp.logical_not(mine))(sems.copy(dst, dst, pieces + 16 * which, pieces + 16 * which + source, mate).wait_recv)

    def drain_pieces(which):
        for m in range(16):
            mine, _, remote = piece(which, m)
            pl.when(jnp.logical_not(mine))(remote.wait_send)

    def right_rings(t):
        return (
            Ring(sems, x, xp, xm, lambda s: rbuf.at[t, z, s, 0], lambda s, h: rbuf.at[t, z, s, 0, pl.ds(32 * h, 32)]),
            Ring(sems, z, zp, zm, lambda s: rbuf.at[t, s, x, 1], lambda s, h: rbuf.at[t, s, x, 1, pl.ds(32 * h, 32)]),
            Ring(sems, z, zp, zm, lambda s: rbuf.at[t, s, :, 0], lambda s, h: rbuf.at[t, s, pl.ds(2 * h, 2), 0]),
            Ring(sems, x, xp, xm, lambda s: rbuf.at[t, :, s, 1], lambda s, h: rbuf.at[t, pl.ds(2 * h, 2), s, 1]),
        )

    def inv_rings(k):
        return (
            Ring(sems, x, xp, xm, lambda s: abuf.at[k, z, s, p, 0], lambda s, h: abuf.at[k, z, s, p, 0, pl.ds(16 * h, 16)],
                 lambda s: None if k == 0 else z >= k),
            Ring(sems, z, zp, zm, lambda s: abuf.at[k, s, x, p, 1], lambda s, h: abuf.at[k, s, x, p, 1, pl.ds(16 * h, 16)],
                 lambda s: None if k == 0 else s >= k),
            Ring(sems, z, zp, zm, lambda s: abuf.at[k, s, :, p, 0], lambda s, h: abuf.at[k, s, pl.ds(2 * h, 2), p, 0],
                 lambda s: None if k == 0 else s >= k),
            Ring(sems, x, xp, xm, lambda s: abuf.at[k, pl.ds(k, 4 - k), s, p, 1],
                 lambda s, h: abuf.at[k, pl.ds(k, 4 - k), s, p, 1, pl.ds(16 * h, 16)]),
        )

    right = [right_rings(t) for t in range(4)]
    inv = [inv_rings(k) for k in range(4)]

    def first_start(group):
        for rings in group:
            rings[0].start()
            rings[1].start()

    def first_forward(group):
        for rings in group:
            rings[0].forward()
            rings[1].forward()

    def second_start(group):
        for rings in group:
            rings[0].finish()
            rings[2].start()
            rings[1].finish()
            rings[3].start()

    def second_forward(group):
        for rings in group:
            rings[2].forward()
            rings[3].forward()

    def second_finish(group):
        for rings in group:
            rings[2].finish()
            rings[3].finish()

    def column_chunk(s):
        return pl.ds(pl.multiple_of(128 * s, 128), 128)

    l_ring = Ring(sems, y, yp, ym, lambda s: lbuf.at[p, :, :, :, column_chunk(s)], lambda s, h: lbuf.at[p, pl.ds(8 * h, 8), :, :, column_chunk(s)])
    w_ring = Ring(sems, y, yp, ym, lambda s: wbuf.at[p, :, column_chunk(s)], lambda s, h: wbuf.at[p, pl.ds(1024 * h, 1024), column_chunk(s)])
    swaps = {"l": sems.take(4), "w": sems.take(4), "a": sems.take(4)}

    def swap(kind, slot, ref):
        return sems.copy(ref, ref, swaps[kind] + slot, swaps[kind] + slot, mate)

    def other(ring, kind, n, owner):
        s = (ring.me, ring.left, ring.right, ring.far)[n]
        buf = lbuf if kind == "l" else wbuf
        ref = buf.at[owner, :, :, :, column_chunk(s)] if kind == "l" else buf.at[owner, :, column_chunk(s)]
        return swap(kind, n, ref)

    def inv_half(k, owner):
        return abuf.at[k, pl.ds(k, 4 - k), :, owner]

    def compute_w():
        for b in range(4):
            acc = None
            for k in range(b + 1):
                term = jnp.dot(abuf[k, b].reshape(512, 512), rjp[4 * k:4 * k + 4].reshape(512, 128), preferred_element_type=F32)
                acc = term if acc is None else acc + term
            sjp[b] = acc.astype(BF)
        for k in range(4):
            acc = None
            for b in range(k, 4):
                term = dot_tn(abuf[k, b].reshape(512, 512), sjp[b])
                acc = term if acc is None else acc + term
            wbuf[p, 512 * k:512 * k + 512, column_chunk(y)] = acc.astype(BF)

    def core_copy(j, t):
        return pltpu.make_async_copy(cores.at[j, t], core_out.at[j, t], local_sem.at[7 + 2 * t + j])

    def compute_core(t):
        rank_i = rank_ref[4 * row + t]
        k_live = lax.broadcasted_iota(jnp.int32, (512, 512), 1) < rank_i

        @pl.loop(0, 2)
        def _(j):
            rank_j = rank_ref[2 * col + j]
            l_live = lax.broadcasted_iota(jnp.int32, (512, 512), 0) < rank_j
            acc = dot_tn(wbuf[j], rbuf[t].reshape(2048, 512))
            cores[j, t] = jnp.where(jnp.logical_and(k_live, l_live), acc, 0.0).astype(BF)

        for j in range(2):
            core_copy(j, t).start()

    left_copy = pltpu.make_async_copy(lbuf, left_out, local_sem.at[15])

    for k in range(4):
        own_inv[k].wait()
    own_right.wait()
    send_pieces(0)
    first_start(inv)
    send_pieces(1)
    first_start(right[:1])
    first_forward(inv)
    second_start(inv)
    first_forward(right[:1])
    first_start(right[1:2])
    take_pieces(1)
    l_ring.start()
    other(l_ring, "l", 0, p).start()
    second_forward(inv)
    second_start(right[:1])
    first_forward(right[1:2])
    first_start(right[2:3])
    second_finish(inv)
    for k in range(4):
        swap("a", k, inv_half(k, p)).start()
    take_pieces(0)
    l_ring.forward()
    for k in range(4):
        swap("a", k, inv_half(k, 1 - p)).wait_recv()
    second_forward(right[:1])
    second_start(right[1:2])
    first_forward(right[2:3])
    first_start(right[3:4])
    compute_w()
    w_ring.start()
    other(w_ring, "w", 0, p).start()
    l_ring.finish()
    for n in range(1, 4):
        other(l_ring, "l", n, p).start()
    second_finish(right[:1])
    second_forward(right[1:2])
    second_start(right[2:3])
    first_forward(right[3:4])
    w_ring.forward()
    second_finish(right[1:2])
    second_forward(right[2:3])
    second_start(right[3:4])
    w_ring.finish()
    for n in range(1, 4):
        other(w_ring, "w", n, p).start()
    for n in range(4):
        other(l_ring, "l", n, 1 - p).wait_recv()
    left_copy.start()
    for n in range(4):
        other(w_ring, "w", n, 1 - p).wait_recv()
    compute_core(0)
    second_finish(right[2:3])
    second_forward(right[3:4])
    compute_core(1)
    compute_core(2)
    second_finish(right[3:4])
    compute_core(3)

    for which in range(2):
        drain_pieces(which)
    for rings in inv + right:
        for ring in rings:
            ring.drain()
    l_ring.drain()
    w_ring.drain()
    for n in range(4):
        other(l_ring, "l", n, p).wait_send()
        other(w_ring, "w", n, p).wait_send()
        swap("a", n, inv_half(n, p)).wait_send()
    left_copy.wait()
    for t in range(4):
        for j in range(2):
            core_copy(j, t).wait()


def gather(pan_left, pan_right, inverse, rank_list):
    return pl.pallas_call(
        gather_kernel,
        out_shape=(jax.ShapeDtypeStruct((2, 4, 512, 512), BF), jax.ShapeDtypeStruct((2, 16, 2, 64, 512), BF)),
        in_specs=[pl.BlockSpec(memory_space=pltpu.VMEM)] * 3 + [pl.BlockSpec(memory_space=pltpu.SMEM)],
        out_specs=(pl.BlockSpec(memory_space=pl.ANY), pl.BlockSpec(memory_space=pl.ANY)),
        scratch_shapes=[
            pltpu.VMEM((4, 4, 4, 2, 64, 512), BF),
            pltpu.VMEM((4, 4, 4, 2, 2, 32, 512), BF),
            pltpu.VMEM((2, 2048, 512), BF),
            pltpu.VMEM((2, 16, 2, 64, 512), BF),
            pltpu.VMEM((16, 2, 64, 128), BF),
            pltpu.VMEM((4, 512, 128), BF),
            pltpu.VMEM((2, 4, 512, 512), BF),
            pltpu.SemaphoreType.DMA((192,)),
            pltpu.SemaphoreType.DMA((192,)),
            pltpu.SemaphoreType.DMA((16,)),
        ],
        compiler_params=pltpu.CompilerParams(collective_id=0, has_side_effects=True, vmem_limit_bytes=60 << 20),
        name="gather",
    )(pan_left.reshape(4, 2, 64, 512), pan_right.reshape(4, 2, 64, 512), inverse.reshape(2, 2, 32, 2048), rank_list)


def update_kernel(core_ref, left_ref, update_ref, gram_ref):
    update = jnp.dot(left_ref[0], core_ref[0, 0], preferred_element_type=F32).astype(BF)
    update_ref[0, 0] = update
    gram_ref[0, 0] = (dot_tn(update_ref[0, 0], update_ref[0, 0]) * (1.0 / 2048)).astype(BF)


def local(pan_left, pan_right, inverse, rank_list):
    core, left = gather(pan_left, pan_right, inverse, rank_list)
    return pl.pallas_call(
        update_kernel,
        grid=(2, 4),
        out_shape=(jax.ShapeDtypeStruct((4, 2, 2048, 512), BF), jax.ShapeDtypeStruct((4, 2, 512, 512), BF)),
        in_specs=[
            pl.BlockSpec((1, 1, 512, 512), lambda j, i: (j, i, 0, 0)),
            pl.BlockSpec((1, 2048, 512), lambda j, i: (j, 0, 0)),
        ],
        out_specs=(
            pl.BlockSpec((1, 1, 2048, 512), lambda j, i: (i, j, 0, 0)),
            pl.BlockSpec((1, 1, 512, 512), lambda j, i: (i, j, 0, 0)),
        ),
        compiler_params=pltpu.CompilerParams(vmem_limit_bytes=48 << 20),
        name="update",
    )(core, left.reshape(2, 2048, 512))


def solution(mesh):
    in_specs = (P("row", "col", None), P("row", "col", None), P("col", None), P())
    out_specs = (P("row", "col", None, None), P("row", "col", None, None))
    return jax.shard_map(local, mesh=mesh, in_specs=in_specs, out_specs=out_specs, check_vma=False)
```

```python
import functools

import jax
import jax.numpy as jnp
from jax import lax
from jax.experimental import pallas as pl
from jax.experimental.pallas import tpu as pltpu
from jax.sharding import PartitionSpec as P

MESH = pl.DeviceIdType.MESH
BF = jnp.bfloat16
F32 = jnp.float32
SPLIT = 80


def device(x, y, z, p):
    return (lax.rem(y, 4) * 2 + p, lax.rem(z, 4) * 4 + lax.rem(x, 4))


def run_if(condition, body):
    if condition is None:
        body()
    else:
        pl.when(condition)(body)


class Semaphores:
    def __init__(self, send, recv):
        self.send, self.recv, self.used = send, recv, 0

    def take(self, count):
        first = self.used
        self.used += count
        return first

    def copy(self, src, dst, send, recv, target):
        return pltpu.make_async_remote_copy(
            src_ref=src, dst_ref=dst, send_sem=self.send.at[send], recv_sem=self.recv.at[recv],
            device_id=target, device_id_type=MESH,
        )


class Ring:
    def __init__(self, sems, me, plus, minus, view, half, has=lambda slot: None):
        self.sems, self.plus, self.minus = sems, plus, minus
        self.view, self.half, self.has = view, half, has
        self.me, self.left, self.right, self.far = me, lax.rem(me + 3, 4), lax.rem(me + 1, 4), lax.rem(me + 2, 4)
        self.base = sems.take(4)

    def message(self, ref, which, target):
        return self.sems.copy(ref, ref, self.base + which, self.base + which, target)

    def start(self):
        def go():
            self.message(self.view(self.me), 0, self.plus).start()
            self.message(self.view(self.me), 1, self.minus).start()

        run_if(self.has(self.me), go)

    def forward(self):
        def from_left():
            self.message(self.view(self.left), 0, self.plus).wait_recv()
            self.message(self.half(self.left, 0), 2, self.plus).start()

        def from_right():
            self.message(self.view(self.right), 1, self.minus).wait_recv()
            self.message(self.half(self.right, 1), 3, self.minus).start()

        run_if(self.has(self.left), from_left)
        run_if(self.has(self.right), from_right)

    def finish(self):
        def go():
            self.message(self.half(self.far, 0), 2, self.plus).wait_recv()
            self.message(self.half(self.far, 1), 3, self.minus).wait_recv()

        run_if(self.has(self.far), go)

    def drain(self):
        def own():
            self.message(self.view(self.me), 0, self.plus).wait_send()
            self.message(self.view(self.me), 1, self.minus).wait_send()

        run_if(self.has(self.me), own)
        run_if(self.has(self.left), lambda: self.message(self.half(self.left, 0), 2, self.plus).wait_send())
        run_if(self.has(self.right), lambda: self.message(self.half(self.right, 1), 3, self.minus).wait_send())


def dot_tn(a, b):
    return lax.dot_general(a, b, (((0,), (0,)), ((), ())), preferred_element_type=F32)


def gather_kernel(
    left_ref, right_ref, inv_ref, rank_ref, cores, left_out, grams,
    rbuf, abuf, wbuf, lbuf, rj, sj, weight, send_sem, recv_sem, local_sem,
):
    row, col = lax.axis_index("row"), lax.axis_index("col")
    x, z, y, p = lax.rem(col, 4), lax.div(col, 4), lax.div(row, 2), lax.rem(row, 2)
    xp, xm = device(x + 1, y, z, p), device(x + 3, y, z, p)
    yp, ym = device(x, y + 1, z, p), device(x, y + 3, z, p)
    zp, zm = device(x, y, z + 1, p), device(x, y, z + 3, p)
    mate = device(x, y, z, 1 - p)
    sems = Semaphores(send_sem, recv_sem)

    own_right = pltpu.make_async_copy(right_ref, rbuf.at[:, z, x], local_sem.at[0])
    own_right.start()
    own_inv = [pltpu.make_async_copy(inv_ref.at[p, :, 512 * k:512 * k + 512], abuf.at[k, z, x, p], local_sem.at[1 + k]) for k in range(4)]
    for k in range(4):
        own_inv[k].start()

    barrier = pltpu.get_barrier_semaphore()
    for target in (xp, xm, yp, ym, zp, zm, mate):
        pl.semaphore_signal(barrier, inc=1, device_id=target, device_id_type=MESH)
    for source in range(16):
        pl.semaphore_signal(barrier, inc=1, device_id=device(source % 4, z, source // 4, lax.div(x, 2)), device_id_type=MESH)
    pl.semaphore_wait(barrier, 23)

    pieces = sems.take(32)
    at_home = jnp.logical_and(y == z, p == lax.div(x, 2))

    def piece(which, m):
        edge, y_to, p_to = m // 8, (m // 2) % 4, m % 2
        x_to = 2 * p + edge
        columns = slice(128 * y_to, 128 * y_to + 128)
        mine = jnp.logical_and(jnp.logical_and(at_home, x_to == x), jnp.logical_and(y_to == y, p_to == p))
        if which == 0:
            src, dst = rbuf.at[2 * edge + p_to, z, x, :, columns], rj.at[col, :, columns]
        else:
            src, dst = left_ref.at[2 * edge + p_to, :, columns], lbuf.at[p_to, col, :, columns]
        remote = sems.copy(src, dst, pieces + 16 * which + m, pieces + 16 * which + col, device(x_to, y_to, y, p_to))
        return mine, pltpu.make_async_copy(src, dst, local_sem.at[5 + which]), remote

    def send_pieces(which):
        for m in range(16):
            mine, local, remote = piece(which, m)
            pl.when(mine)(local.start)
            pl.when(jnp.logical_not(mine))(remote.start)

    def take_pieces(which):
        ycol = pl.ds(pl.multiple_of(128 * y, 128), 128)
        for source in range(16):
            dst = rj.at[source, :, ycol] if which == 0 else lbuf.at[p, source, :, ycol]
            mine = jnp.logical_and(at_home, col == source)
            pl.when(mine)(pltpu.make_async_copy(dst, dst, local_sem.at[5 + which]).wait)
            pl.when(jnp.logical_not(mine))(sems.copy(dst, dst, pieces + 16 * which, pieces + 16 * which + source, mate).wait_recv)

    def drain_pieces(which):
        for m in range(16):
            mine, _, remote = piece(which, m)
            pl.when(jnp.logical_not(mine))(remote.wait_send)

    first, second = pl.ds(0, SPLIT), pl.ds(SPLIT, 128 - SPLIT)

    def side(h):
        return pl.ds(256 * h, 256)

    def right_rings(t):
        return (
            Ring(sems, x, xp, xm, lambda s: rbuf.at[t, z, s, first], lambda s, h: rbuf.at[t, z, s, first, side(h)]),
            Ring(sems, z, zp, zm, lambda s: rbuf.at[t, s, x, second], lambda s, h: rbuf.at[t, s, x, second, side(h)]),
            Ring(sems, z, zp, zm, lambda s: rbuf.at[t, s, :, first], lambda s, h: rbuf.at[t, s, pl.ds(2 * h, 2), first]),
            Ring(sems, x, xp, xm, lambda s: rbuf.at[t, :, s, second], lambda s, h: rbuf.at[t, pl.ds(2 * h, 2), s, second]),
        )

    def inv_rings(k):
        return (
            Ring(sems, z, zp, zm, lambda s: abuf.at[k, s, x, p], lambda s, h: abuf.at[k, s, x, p, pl.ds(32 * h, 32)],
                 lambda s: None if k == 0 else s >= k),
            Ring(sems, x, xp, xm, lambda s: abuf.at[k, pl.ds(k, 4 - k), s, p],
                 lambda s, h: abuf.at[k, pl.ds(k, 4 - k), s, p, pl.ds(32 * h, 32)]),
        )

    right = [right_rings(t) for t in range(4)]
    inv = [inv_rings(k) for k in range(4)]

    def start(stage, tiles):
        for t in tiles:
            right[t][stage].start()

    def forward(stage, tiles):
        for t in tiles:
            right[t][stage].forward()

    def finish(stage, tiles):
        for t in tiles:
            right[t][stage].finish()

    def turn(stage, tiles):
        finish(stage, tiles)
        start(stage + 2, tiles)

    def inv_first():
        for ring, _ in inv:
            ring.start()

    def inv_first_forward():
        for ring, _ in inv:
            ring.forward()

    def inv_turn():
        for first_ring, second_ring in inv:
            first_ring.finish()
            second_ring.start()

    def inv_second_forward():
        for _, ring in inv:
            ring.forward()

    def inv_second_finish():
        for _, ring in inv:
            ring.finish()

    def column_chunk(s):
        return pl.ds(pl.multiple_of(128 * s, 128), 128)

    l_ring = Ring(sems, y, yp, ym, lambda s: lbuf.at[p, :, :, column_chunk(s)], lambda s, h: lbuf.at[p, pl.ds(8 * h, 8), :, column_chunk(s)])
    r_ring = Ring(sems, y, yp, ym, lambda s: rj.at[:, :, column_chunk(s)], lambda s, h: rj.at[pl.ds(8 * h, 8), :, column_chunk(s)])
    swaps = {"l": sems.take(4), "w": sems.take(4), "a": sems.take(4)}

    def swap(kind, slot, ref):
        return sems.copy(ref, ref, swaps[kind] + slot, swaps[kind] + slot, mate)

    def left_swap(n, owner):
        s = (l_ring.me, l_ring.left, l_ring.right, l_ring.far)[n]
        return swap("l", n, lbuf.at[owner, :, :, column_chunk(s)])

    def inv_swap(k, owner):
        return swap("a", k, abuf.at[k, pl.ds(k, 4 - k), :, owner])

    def w_swap(k, owner):
        return swap("w", k, wbuf.at[owner, 512 * k:512 * k + 512])

    def compute_s():
        for b in range(4):
            acc = None
            for k in range(b + 1):
                term = jnp.dot(abuf[k, b].reshape(512, 512), rj[4 * k:4 * k + 4].reshape(512, 512), preferred_element_type=F32)
                acc = term if acc is None else acc + term
            sj[b] = acc.astype(BF)

    def compute_w():
        for k in range(4):
            acc = None
            for b in range(k, 4):
                term = dot_tn(abuf[k, b].reshape(512, 512), sj[b])
                acc = term if acc is None else acc + term
            wbuf[p, 512 * k:512 * k + 512] = acc.astype(BF)

    def compute_core(t, n):
        j = p if n == 0 else 1 - p
        k_live = lax.broadcasted_iota(jnp.int32, (512, 512), 1) < rank_ref[4 * row + t]
        l_live = lax.broadcasted_iota(jnp.int32, (512, 512), 0) < rank_ref[2 * col + j]
        acc = dot_tn(wbuf[j], rbuf[t].reshape(2048, 512))
        cores[j, t] = jnp.where(jnp.logical_and(k_live, l_live), acc, 0.0).astype(BF)

    def compute_weight():
        @pl.loop(0, 2)
        def _(j):
            factor = lbuf[j].reshape(2048, 512)
            weight[j] = (dot_tn(factor, factor) * (1.0 / 2048)).astype(BF)

    def compute_gram(t):
        @pl.loop(0, 2)
        def _(j):
            core = cores[j, t]
            half = jnp.dot(weight[j], core, preferred_element_type=F32).astype(BF)
            grams[t, j] = dot_tn(core, half).astype(BF)

    left_copy = pltpu.make_async_copy(lbuf, left_out, local_sem.at[7])

    def l_start():
        l_ring.start()
        left_swap(0, p).start()

    def l_finish():
        l_ring.finish()
        for n in range(1, 4):
            left_swap(n, p).start()

    def l_take():
        for n in range(4):
            left_swap(n, 1 - p).wait_recv()
        left_copy.start()

    def inv_send():
        for k in range(4):
            inv_swap(k, p).start()

    def inv_take():
        for k in range(4):
            inv_swap(k, 1 - p).wait_recv()

    def w_send():
        for k in range(4):
            w_swap(k, p).start()

    def w_take():
        for k in range(4):
            w_swap(k, 1 - p).wait_recv()

    def drain_early():
        for which in range(2):
            drain_pieces(which)
        for rings in inv:
            for ring in rings:
                ring.drain()
        for t in range(4):
            right[t][0].drain()
            right[t][1].drain()
        r_ring.drain()
        for k in range(4):
            inv_swap(k, p).wait_send()
            w_swap(k, p).wait_send()

    def drain_left():
        l_ring.drain()
        for k in range(4):
            left_swap(k, p).wait_send()

    for k in range(4):
        own_inv[k].wait()
    own_right.wait()
    inv_first()
    send_pieces(0)
    start(0, (0, 1))
    inv_first_forward()
    forward(0, (0, 1))
    inv_turn()
    start(1, range(4))
    take_pieces(0)
    r_ring.start()
    turn(0, (0, 1))
    forward(1, range(4))
    r_ring.forward()
    inv_second_forward()
    start(0, (2, 3))
    send_pieces(1)
    forward(2, (0,))
    forward(0, (2, 3))
    inv_second_finish()
    inv_send()
    turn(1, (0,))
    r_ring.finish()
    inv_take()
    compute_s()
    take_pieces(1)
    l_start()
    forward(2, (1,))
    turn(0, (2, 3))
    turn(1, (1,))
    compute_w()
    w_send()
    forward(3, (0,))
    l_ring.forward()
    turn(1, (2,))
    finish(2, (0, 1))
    finish(3, (0,))
    compute_core(0, 0)
    forward(3, (1,))
    w_take()
    compute_core(0, 1)
    forward(2, (2, 3))
    turn(1, (3,))
    l_finish()
    finish(3, (1,))
    compute_core(1, 0)
    compute_core(1, 1)
    drain_early()
    forward(3, (2,))
    l_take()
    compute_weight()
    forward(3, (3,))
    compute_gram(0)
    compute_gram(1)
    drain_left()
    finish(2, (2,))
    finish(3, (2,))
    compute_core(2, 0)
    compute_core(2, 1)
    compute_gram(2)
    finish(2, (3,))
    finish(3, (3,))
    compute_core(3, 0)
    compute_core(3, 1)
    compute_gram(3)
    for t in range(4):
        right[t][2].drain()
        right[t][3].drain()
    left_copy.wait()


def gather(pan_left, pan_right, inverse, rank_list):
    return pl.pallas_call(
        gather_kernel,
        out_shape=(
            pltpu.VMEM((2, 4, 512, 512), BF), pltpu.VMEM((2, 16, 128, 512), BF), pltpu.VMEM((4, 2, 512, 512), BF),
        ),
        in_specs=[pl.BlockSpec(memory_space=pltpu.HBM)] * 3 + [pl.BlockSpec(memory_space=pltpu.SMEM)],
        out_specs=[pl.BlockSpec(memory_space=pltpu.VMEM)] * 3,
        scratch_shapes=[
            pltpu.VMEM((4, 4, 4, 128, 512), BF),
            pltpu.VMEM((4, 4, 4, 2, 64, 512), BF),
            pltpu.VMEM((2, 2048, 512), BF),
            pltpu.VMEM((2, 16, 128, 512), BF),
            pltpu.VMEM((16, 128, 512), BF),
            pltpu.VMEM((4, 512, 512), BF),
            pltpu.VMEM((2, 512, 512), BF),
            pltpu.SemaphoreType.DMA((192,)),
            pltpu.SemaphoreType.DMA((192,)),
            pltpu.SemaphoreType.DMA((8,)),
        ],
        compiler_params=pltpu.CompilerParams(collective_id=0, has_side_effects=True, vmem_limit_bytes=54329344),
        name="gather",
    )(pan_left, pan_right, inverse.reshape(2, 64, 2048), rank_list)


def update_kernel(core_ref, left_ref, gram_in, update_ref, gram_ref):
    j, i = pl.program_id(0), pl.program_id(1)
    update_ref[0, 0] = jnp.dot(left_ref[j].reshape(2048, 512), core_ref[j, i], preferred_element_type=F32).astype(BF)
    gram_ref[0, 0] = gram_in[i, j]


def local(pan_left, pan_right, inverse, rank_list):
    core, left, gram = gather(pan_left, pan_right, inverse, rank_list)
    return pl.pallas_call(
        update_kernel,
        grid=(2, 4),
        out_shape=(jax.ShapeDtypeStruct((4, 2, 2048, 512), BF), jax.ShapeDtypeStruct((4, 2, 512, 512), BF)),
        in_specs=[pl.BlockSpec(memory_space=pltpu.VMEM)] * 3,
        out_specs=(
            pl.BlockSpec((1, 1, 2048, 512), lambda j, i: (i, j, 0, 0)),
            pl.BlockSpec((1, 1, 512, 512), lambda j, i: (i, j, 0, 0)),
        ),
        compiler_params=pltpu.CompilerParams(vmem_limit_bytes=24 << 20),
        name="update",
    )(core, left, gram)


def solution(mesh):
    in_specs = (P("row", "col", None), P("row", "col", None), P("col", None), P())
    out_specs = (P("row", "col", None, None), P("row", "col", None, None))
    return jax.shard_map(local, mesh=mesh, in_specs=in_specs, out_specs=out_specs, check_vma=False)
```

```python
import functools

import jax
import jax.numpy as jnp
from jax import lax
from jax.experimental import pallas as pl
from jax.experimental.pallas import tpu as pltpu
from jax.sharding import PartitionSpec as P

MESH = pl.DeviceIdType.MESH
BF = jnp.bfloat16
F32 = jnp.float32
SPLIT = 80


def device(x, y, z, p):
    return (lax.rem(y, 4) * 2 + p, lax.rem(z, 4) * 4 + lax.rem(x, 4))


def run_if(condition, body):
    if condition is None:
        body()
    else:
        pl.when(condition)(body)


class Semaphores:
    def __init__(self, send, recv):
        self.send, self.recv, self.used = send, recv, 0

    def take(self, count):
        first = self.used
        self.used += count
        return first

    def copy(self, src, dst, send, recv, target):
        return pltpu.make_async_remote_copy(
            src_ref=src, dst_ref=dst, send_sem=self.send.at[send], recv_sem=self.recv.at[recv],
            device_id=target, device_id_type=MESH,
        )


class Ring:
    def __init__(self, sems, me, plus, minus, view, half, has=lambda slot: None):
        self.sems, self.plus, self.minus = sems, plus, minus
        self.view, self.half, self.has = view, half, has
        self.me, self.left, self.right, self.far = me, lax.rem(me + 3, 4), lax.rem(me + 1, 4), lax.rem(me + 2, 4)
        self.base = sems.take(4)

    def message(self, ref, which, target):
        return self.sems.copy(ref, ref, self.base + which, self.base + which, target)

    def start(self):
        def go():
            self.message(self.view(self.me), 0, self.plus).start()
            self.message(self.view(self.me), 1, self.minus).start()

        run_if(self.has(self.me), go)

    def forward(self):
        def from_left():
            self.message(self.view(self.left), 0, self.plus).wait_recv()
            self.message(self.half(self.left, 0), 2, self.plus).start()

        def from_right():
            self.message(self.view(self.right), 1, self.minus).wait_recv()
            self.message(self.half(self.right, 1), 3, self.minus).start()

        run_if(self.has(self.left), from_left)
        run_if(self.has(self.right), from_right)

    def finish(self):
        def go():
            self.message(self.half(self.far, 0), 2, self.plus).wait_recv()
            self.message(self.half(self.far, 1), 3, self.minus).wait_recv()

        run_if(self.has(self.far), go)

    def drain(self):
        def own():
            self.message(self.view(self.me), 0, self.plus).wait_send()
            self.message(self.view(self.me), 1, self.minus).wait_send()

        run_if(self.has(self.me), own)
        run_if(self.has(self.left), lambda: self.message(self.half(self.left, 0), 2, self.plus).wait_send())
        run_if(self.has(self.right), lambda: self.message(self.half(self.right, 1), 3, self.minus).wait_send())


def dot_tn(a, b):
    return lax.dot_general(a, b, (((0,), (0,)), ((), ())), preferred_element_type=F32)


def gather_kernel(
    left_ref, right_ref, inv_ref, rank_ref, cores, lbuf, grams,
    rbuf, abuf, wbuf, rj, sj, weight, send_sem, recv_sem, local_sem,
):
    row, col = lax.axis_index("row"), lax.axis_index("col")
    x, z, y, p = lax.rem(col, 4), lax.div(col, 4), lax.div(row, 2), lax.rem(row, 2)
    xp, xm = device(x + 1, y, z, p), device(x + 3, y, z, p)
    yp, ym = device(x, y + 1, z, p), device(x, y + 3, z, p)
    zp, zm = device(x, y, z + 1, p), device(x, y, z + 3, p)
    mate = device(x, y, z, 1 - p)
    sems = Semaphores(send_sem, recv_sem)

    own_right = pltpu.make_async_copy(right_ref, rbuf.at[:, z, x], local_sem.at[0])
    own_right.start()
    own_inv = [pltpu.make_async_copy(inv_ref.at[p, :, 512 * k:512 * k + 512], abuf.at[k, z, x, p], local_sem.at[1 + k]) for k in range(4)]
    for k in range(4):
        own_inv[k].start()

    barrier = pltpu.get_barrier_semaphore()
    for target in (xp, xm, yp, ym, zp, zm, mate):
        pl.semaphore_signal(barrier, inc=1, device_id=target, device_id_type=MESH)
    for source in range(16):
        pl.semaphore_signal(barrier, inc=1, device_id=device(source % 4, z, source // 4, lax.div(x, 2)), device_id_type=MESH)
    pl.semaphore_wait(barrier, 23)

    pieces = sems.take(32)
    at_home = jnp.logical_and(y == z, p == lax.div(x, 2))

    def piece(which, m):
        edge, y_to, p_to = m // 8, (m // 2) % 4, m % 2
        x_to = 2 * p + edge
        columns = slice(128 * y_to, 128 * y_to + 128)
        mine = jnp.logical_and(jnp.logical_and(at_home, x_to == x), jnp.logical_and(y_to == y, p_to == p))
        if which == 0:
            src, dst = rbuf.at[2 * edge + p_to, z, x, :, columns], rj.at[col, :, columns]
        else:
            src, dst = left_ref.at[2 * edge + p_to, :, columns], lbuf.at[p_to, col, :, columns]
        remote = sems.copy(src, dst, pieces + 16 * which + m, pieces + 16 * which + col, device(x_to, y_to, y, p_to))
        return mine, pltpu.make_async_copy(src, dst, local_sem.at[5 + which]), remote

    def send_pieces(which):
        for m in range(16):
            mine, local, remote = piece(which, m)
            pl.when(mine)(local.start)
            pl.when(jnp.logical_not(mine))(remote.start)

    def take_pieces(which):
        ycol = pl.ds(pl.multiple_of(128 * y, 128), 128)
        for source in range(16):
            dst = rj.at[source, :, ycol] if which == 0 else lbuf.at[p, source, :, ycol]
            mine = jnp.logical_and(at_home, col == source)
            pl.when(mine)(pltpu.make_async_copy(dst, dst, local_sem.at[5 + which]).wait)
            pl.when(jnp.logical_not(mine))(sems.copy(dst, dst, pieces + 16 * which, pieces + 16 * which + source, mate).wait_recv)

    def drain_pieces(which):
        for m in range(16):
            mine, _, remote = piece(which, m)
            pl.when(jnp.logical_not(mine))(remote.wait_send)

    first, second = pl.ds(0, SPLIT), pl.ds(SPLIT, 128 - SPLIT)

    def side(h):
        return pl.ds(256 * h, 256)

    def right_rings(t):
        return (
            Ring(sems, x, xp, xm, lambda s: rbuf.at[t, z, s, first], lambda s, h: rbuf.at[t, z, s, first, side(h)]),
            Ring(sems, z, zp, zm, lambda s: rbuf.at[t, s, x, second], lambda s, h: rbuf.at[t, s, x, second, side(h)]),
            Ring(sems, z, zp, zm, lambda s: rbuf.at[t, s, :, first], lambda s, h: rbuf.at[t, s, pl.ds(2 * h, 2), first]),
            Ring(sems, x, xp, xm, lambda s: rbuf.at[t, :, s, second], lambda s, h: rbuf.at[t, pl.ds(2 * h, 2), s, second]),
        )

    def inv_rings(k):
        return (
            Ring(sems, z, zp, zm, lambda s: abuf.at[k, s, x, p], lambda s, h: abuf.at[k, s, x, p, pl.ds(32 * h, 32)],
                 lambda s: None if k == 0 else s >= k),
            Ring(sems, x, xp, xm, lambda s: abuf.at[k, pl.ds(k, 4 - k), s, p],
                 lambda s, h: abuf.at[k, pl.ds(k, 4 - k), s, p, pl.ds(32 * h, 32)]),
        )

    right = [right_rings(t) for t in range(4)]
    inv = [inv_rings(k) for k in range(4)]

    def start(stage, tiles):
        for t in tiles:
            right[t][stage].start()

    def forward(stage, tiles):
        for t in tiles:
            right[t][stage].forward()

    def finish(stage, tiles):
        for t in tiles:
            right[t][stage].finish()

    def turn(stage, tiles):
        finish(stage, tiles)
        start(stage + 2, tiles)

    def inv_first():
        for ring, _ in inv:
            ring.start()

    def inv_first_forward():
        for ring, _ in inv:
            ring.forward()

    def inv_turn():
        for first_ring, second_ring in inv:
            first_ring.finish()
            second_ring.start()

    def inv_second_forward():
        for _, ring in inv:
            ring.forward()

    def inv_second_finish():
        for _, ring in inv:
            ring.finish()

    def column_chunk(s):
        return pl.ds(pl.multiple_of(128 * s, 128), 128)

    l_ring = Ring(sems, y, yp, ym, lambda s: lbuf.at[p, :, :, column_chunk(s)], lambda s, h: lbuf.at[p, pl.ds(8 * h, 8), :, column_chunk(s)])
    r_ring = Ring(sems, y, yp, ym, lambda s: rj.at[:, :, column_chunk(s)], lambda s, h: rj.at[pl.ds(8 * h, 8), :, column_chunk(s)])
    swaps = {"l": sems.take(4), "w": sems.take(4), "a": sems.take(16), "g": sems.take(1)}

    def swap(kind, slot, ref):
        return sems.copy(ref, ref, swaps[kind] + slot, swaps[kind] + slot, mate)

    def left_swap(n, owner):
        s = (l_ring.me, l_ring.left, l_ring.right, l_ring.far)[n]
        return swap("l", n, lbuf.at[owner, :, :, column_chunk(s)])

    def inv_swap(k, n, owner):
        slot = lax.rem(x + n, 4)
        return swap("a", 4 * k + n, abuf.at[k, pl.ds(k, 4 - k), slot, owner])

    def inv_send(*slots):
        for n in slots:
            for k in range(4):
                inv_swap(k, n, p).start()

    def weight_swap(owner):
        return swap("g", 0, weight.at[owner])

    def w_swap(k, owner):
        return swap("w", k, wbuf.at[owner, 512 * k:512 * k + 512])

    def compute_s():
        for b in range(4):
            acc = None
            for k in range(b + 1):
                term = jnp.dot(abuf[k, b].reshape(512, 512), rj[4 * k:4 * k + 4].reshape(512, 512), preferred_element_type=F32)
                acc = term if acc is None else acc + term
            sj[b] = acc.astype(BF)

    def compute_w():
        for k in range(4):
            acc = None
            for b in range(k, 4):
                term = dot_tn(abuf[k, b].reshape(512, 512), sj[b])
                acc = term if acc is None else acc + term
            wbuf[p, 512 * k:512 * k + 512] = acc.astype(BF)

    def compute_core(t, n):
        j = p if n == 0 else 1 - p
        k_live = lax.broadcasted_iota(jnp.int32, (512, 512), 1) < rank_ref[4 * row + t]
        l_live = lax.broadcasted_iota(jnp.int32, (512, 512), 0) < rank_ref[2 * col + j]
        acc = dot_tn(wbuf[j], rbuf[t].reshape(2048, 512))
        cores[j, t] = jnp.where(jnp.logical_and(k_live, l_live), acc, 0.0).astype(BF)

    def compute_weight():
        factor = lbuf[p].reshape(2048, 512)
        weight[p] = (dot_tn(factor, factor) * (1.0 / 2048)).astype(BF)

    def compute_gram(t):
        @pl.loop(0, 2)
        def _(j):
            core = cores[j, t]
            half = jnp.dot(weight[j], core, preferred_element_type=F32).astype(BF)
            grams[t, j] = dot_tn(core, half).astype(BF)

    def l_start():
        l_ring.start()
        left_swap(0, p).start()

    def l_finish():
        l_ring.finish()
        for n in range(1, 4):
            left_swap(n, p).start()

    def l_take():
        for n in range(4):
            left_swap(n, 1 - p).wait_recv()

    def inv_take():
        for k in range(4):
            for n in range(4):
                inv_swap(k, n, 1 - p).wait_recv()

    def w_send():
        for k in range(4):
            w_swap(k, p).start()

    def w_take():
        for k in range(4):
            w_swap(k, 1 - p).wait_recv()

    def drain_early():
        for which in range(2):
            drain_pieces(which)
        for rings in inv:
            for ring in rings:
                ring.drain()
        for t in range(4):
            right[t][0].drain()
            right[t][1].drain()
        r_ring.drain()
        for k in range(4):
            for n in range(4):
                inv_swap(k, n, p).wait_send()
            w_swap(k, p).wait_send()

    def drain_left():
        weight_swap(p).wait_send()
        l_ring.drain()
        for k in range(4):
            left_swap(k, p).wait_send()

    for k in range(4):
        own_inv[k].wait()
    own_right.wait()
    inv_first()
    send_pieces(0)
    send_pieces(1)
    start(0, range(4))
    inv_first_forward()
    forward(0, range(4))
    inv_turn()
    inv_send(0)
    start(1, range(4))
    take_pieces(0)
    r_ring.start()
    turn(0, (0, 1))
    forward(1, range(4))
    r_ring.forward()
    take_pieces(1)
    l_start()
    inv_second_forward()
    inv_send(1, 3)
    turn(0, (2,))
    forward(2, (0, 1))
    turn(1, (0,))
    turn(0, (3,))
    inv_second_finish()
    inv_send(2)
    turn(1, (1, 2))
    r_ring.finish()
    inv_take()
    compute_s()
    forward(2, (2,))
    forward(3, (0,))
    turn(1, (3,))
    l_ring.forward()
    compute_w()
    w_send()
    finish(2, (0, 1))
    finish(3, (0,))
    forward(3, (1,))
    compute_core(0, 0)
    w_take()
    compute_core(0, 1)
    l_finish()
    forward(2, (3,))
    forward(3, (2,))
    finish(3, (1,))
    compute_weight()
    compute_core(1, 0)
    forward(3, (3,))
    compute_core(1, 1)
    weight_swap(p).start()
    finish(2, (2,))
    finish(3, (2,))
    compute_core(2, 0)
    compute_core(2, 1)
    weight_swap(1 - p).wait_recv()
    compute_gram(0)
    compute_gram(1)
    drain_early()
    compute_gram(2)
    finish(2, (3,))
    finish(3, (3,))
    l_take()
    drain_left()
    compute_core(3, 0)
    compute_core(3, 1)
    compute_gram(3)
    for t in range(4):
        right[t][2].drain()
        right[t][3].drain()


def gather(pan_left, pan_right, inverse, rank_list):
    return pl.pallas_call(
        gather_kernel,
        out_shape=(
            pltpu.VMEM((2, 4, 512, 512), BF), pltpu.VMEM((2, 16, 128, 512), BF), pltpu.VMEM((4, 2, 512, 512), BF),
        ),
        in_specs=[pl.BlockSpec(memory_space=pltpu.HBM)] * 3 + [pl.BlockSpec(memory_space=pltpu.SMEM)],
        out_specs=[pl.BlockSpec(memory_space=pltpu.VMEM)] * 3,
        scratch_shapes=[
            pltpu.VMEM((4, 4, 4, 128, 512), BF),
            pltpu.VMEM((4, 4, 4, 2, 64, 512), BF),
            pltpu.VMEM((2, 2048, 512), BF),
            pltpu.VMEM((16, 128, 512), BF),
            pltpu.VMEM((4, 512, 512), BF),
            pltpu.VMEM((2, 512, 512), BF),
            pltpu.SemaphoreType.DMA((161,)),
            pltpu.SemaphoreType.DMA((161,)),
            pltpu.SemaphoreType.DMA((7,)),
        ],
        compiler_params=pltpu.CompilerParams(collective_id=0, has_side_effects=True, vmem_limit_bytes=54329344),
        name="gather",
    )(pan_left, pan_right, inverse.reshape(2, 64, 2048), rank_list)


def update_kernel(core_ref, left_ref, gram_in, update_ref, gram_ref):
    j, i = pl.program_id(0), pl.program_id(1)
    update_ref[0, 0] = jnp.dot(left_ref[j].reshape(2048, 512), core_ref[j, i], preferred_element_type=F32).astype(BF)
    gram_ref[0, 0] = gram_in[i, j]


def local(pan_left, pan_right, inverse, rank_list):
    core, left, gram = gather(pan_left, pan_right, inverse, rank_list)
    return pl.pallas_call(
        update_kernel,
        grid=(2, 4),
        out_shape=(jax.ShapeDtypeStruct((4, 2, 2048, 512), BF), jax.ShapeDtypeStruct((4, 2, 512, 512), BF)),
        in_specs=[pl.BlockSpec(memory_space=pltpu.VMEM)] * 3,
        out_specs=(
            pl.BlockSpec((1, 1, 2048, 512), lambda j, i: (i, j, 0, 0)),
            pl.BlockSpec((1, 1, 512, 512), lambda j, i: (i, j, 0, 0)),
        ),
        compiler_params=pltpu.CompilerParams(vmem_limit_bytes=24 << 20),
        name="update",
    )(core, left, gram)


def solution(mesh):
    in_specs = (P("row", "col", None), P("row", "col", None), P("col", None), P())
    out_specs = (P("row", "col", None, None), P("row", "col", None, None))
    return jax.shard_map(local, mesh=mesh, in_specs=in_specs, out_specs=out_specs, check_vma=False)
```

```python
import functools

import jax
import jax.numpy as jnp
from jax import lax
from jax.experimental import pallas as pl
from jax.experimental.pallas import tpu as pltpu
from jax.sharding import PartitionSpec as P

MESH = pl.DeviceIdType.MESH
BF = jnp.bfloat16
F32 = jnp.float32
SPLIT = 80


def device(x, y, z, p):
    return (lax.rem(y, 4) * 2 + p, lax.rem(z, 4) * 4 + lax.rem(x, 4))


def run_if(condition, body):
    if condition is None:
        body()
    else:
        pl.when(condition)(body)


class Semaphores:
    def __init__(self, send, recv):
        self.send, self.recv, self.used = send, recv, 0

    def take(self, count):
        first = self.used
        self.used += count
        return first

    def copy(self, src, dst, send, recv, target):
        return pltpu.make_async_remote_copy(
            src_ref=src, dst_ref=dst, send_sem=self.send.at[send], recv_sem=self.recv.at[recv],
            device_id=target, device_id_type=MESH,
        )


class Ring:
    def __init__(self, sems, me, plus, minus, view, half, has=lambda slot: None):
        self.sems, self.plus, self.minus = sems, plus, minus
        self.view, self.half, self.has = view, half, has
        self.me, self.left, self.right, self.far = me, lax.rem(me + 3, 4), lax.rem(me + 1, 4), lax.rem(me + 2, 4)
        self.base = sems.take(4)

    def message(self, ref, which, target):
        return self.sems.copy(ref, ref, self.base + which, self.base + which, target)

    def start(self):
        def go():
            self.message(self.view(self.me), 0, self.plus).start()
            self.message(self.view(self.me), 1, self.minus).start()

        run_if(self.has(self.me), go)

    def forward(self):
        def from_left():
            self.message(self.view(self.left), 0, self.plus).wait_recv()
            self.message(self.half(self.left, 0), 2, self.plus).start()

        def from_right():
            self.message(self.view(self.right), 1, self.minus).wait_recv()
            self.message(self.half(self.right, 1), 3, self.minus).start()

        run_if(self.has(self.left), from_left)
        run_if(self.has(self.right), from_right)

    def finish(self):
        def go():
            self.message(self.half(self.far, 0), 2, self.plus).wait_recv()
            self.message(self.half(self.far, 1), 3, self.minus).wait_recv()

        run_if(self.has(self.far), go)

    def drain(self):
        def own():
            self.message(self.view(self.me), 0, self.plus).wait_send()
            self.message(self.view(self.me), 1, self.minus).wait_send()

        run_if(self.has(self.me), own)
        run_if(self.has(self.left), lambda: self.message(self.half(self.left, 0), 2, self.plus).wait_send())
        run_if(self.has(self.right), lambda: self.message(self.half(self.right, 1), 3, self.minus).wait_send())


def dot_tn(a, b):
    return lax.dot_general(a, b, (((0,), (0,)), ((), ())), preferred_element_type=F32)


def gather_kernel(
    left_ref, right_ref, inv_ref, rank_ref, cores, lbuf, grams,
    rbuf, abuf, wbuf, rj, sj, weight, send_sem, recv_sem, local_sem,
):
    row, col = lax.axis_index("row"), lax.axis_index("col")
    x, z, y, p = lax.rem(col, 4), lax.div(col, 4), lax.div(row, 2), lax.rem(row, 2)
    xp, xm = device(x + 1, y, z, p), device(x + 3, y, z, p)
    yp, ym = device(x, y + 1, z, p), device(x, y + 3, z, p)
    zp, zm = device(x, y, z + 1, p), device(x, y, z + 3, p)
    mate = device(x, y, z, 1 - p)
    sems = Semaphores(send_sem, recv_sem)

    own_right = pltpu.make_async_copy(right_ref, rbuf.at[:, z, x], local_sem.at[0])
    own_right.start()
    own_inv = [pltpu.make_async_copy(inv_ref.at[p, :, 512 * k:512 * k + 512], abuf.at[k, z, x, p], local_sem.at[1 + k]) for k in range(4)]
    for k in range(4):
        own_inv[k].start()

    barrier = pltpu.get_barrier_semaphore()
    for target in (xp, xm, yp, ym, zp, zm, mate):
        pl.semaphore_signal(barrier, inc=1, device_id=target, device_id_type=MESH)
    for source in range(16):
        pl.semaphore_signal(barrier, inc=1, device_id=device(source % 4, z, source // 4, lax.div(x, 2)), device_id_type=MESH)
    pl.semaphore_wait(barrier, 23)

    pieces = sems.take(32)
    at_home = jnp.logical_and(y == z, p == lax.div(x, 2))

    def piece(which, m):
        edge, y_to, p_to = m // 8, (m // 2) % 4, m % 2
        x_to = 2 * p + edge
        columns = slice(128 * y_to, 128 * y_to + 128)
        mine = jnp.logical_and(jnp.logical_and(at_home, x_to == x), jnp.logical_and(y_to == y, p_to == p))
        if which == 0:
            src, dst = rbuf.at[2 * edge + p_to, z, x, :, columns], rj.at[col, :, columns]
        else:
            src, dst = left_ref.at[2 * edge + p_to, :, columns], lbuf.at[p_to, col, :, columns]
        remote = sems.copy(src, dst, pieces + 16 * which + m, pieces + 16 * which + col, device(x_to, y_to, y, p_to))
        return mine, pltpu.make_async_copy(src, dst, local_sem.at[5 + which]), remote

    def send_pieces(which):
        for m in range(16):
            mine, local, remote = piece(which, m)
            pl.when(mine)(local.start)
            pl.when(jnp.logical_not(mine))(remote.start)

    def take_pieces(which):
        ycol = pl.ds(pl.multiple_of(128 * y, 128), 128)
        for source in range(16):
            dst = rj.at[source, :, ycol] if which == 0 else lbuf.at[p, source, :, ycol]
            mine = jnp.logical_and(at_home, col == source)
            pl.when(mine)(pltpu.make_async_copy(dst, dst, local_sem.at[5 + which]).wait)
            pl.when(jnp.logical_not(mine))(sems.copy(dst, dst, pieces + 16 * which, pieces + 16 * which + source, mate).wait_recv)

    def drain_pieces(which):
        for m in range(16):
            mine, _, remote = piece(which, m)
            pl.when(jnp.logical_not(mine))(remote.wait_send)

    first, second = pl.ds(0, SPLIT), pl.ds(SPLIT, 128 - SPLIT)

    def side(h):
        return pl.ds(256 * h, 256)

    def right_rings(t):
        return (
            Ring(sems, x, xp, xm, lambda s: rbuf.at[t, z, s, first], lambda s, h: rbuf.at[t, z, s, first, side(h)]),
            Ring(sems, z, zp, zm, lambda s: rbuf.at[t, s, x, second], lambda s, h: rbuf.at[t, s, x, second, side(h)]),
            Ring(sems, z, zp, zm, lambda s: rbuf.at[t, s, :, first], lambda s, h: rbuf.at[t, s, pl.ds(2 * h, 2), first]),
            Ring(sems, x, xp, xm, lambda s: rbuf.at[t, :, s, second], lambda s, h: rbuf.at[t, pl.ds(2 * h, 2), s, second]),
        )

    def inv_rings(k):
        return (
            Ring(sems, z, zp, zm, lambda s: abuf.at[k, s, x, p], lambda s, h: abuf.at[k, s, x, p, pl.ds(32 * h, 32)],
                 lambda s: None if k == 0 else s >= k),
            Ring(sems, x, xp, xm, lambda s: abuf.at[k, pl.ds(k, 4 - k), s, p],
                 lambda s, h: abuf.at[k, pl.ds(k, 4 - k), s, p, pl.ds(32 * h, 32)]),
        )

    right = [right_rings(t) for t in range(4)]
    inv = [inv_rings(k) for k in range(4)]

    def start(stage, tiles):
        for t in tiles:
            right[t][stage].start()

    def forward(stage, tiles):
        for t in tiles:
            right[t][stage].forward()

    def finish(stage, tiles):
        for t in tiles:
            right[t][stage].finish()

    def turn(stage, tiles):
        finish(stage, tiles)
        start(stage + 2, tiles)

    def inv_first():
        for ring, _ in inv:
            ring.start()

    def inv_first_forward():
        for ring, _ in inv:
            ring.forward()

    def inv_turn():
        for first_ring, second_ring in inv:
            first_ring.finish()
            second_ring.start()

    def inv_second_forward():
        for _, ring in inv:
            ring.forward()

    def inv_second_finish():
        for _, ring in inv:
            ring.finish()

    def column_chunk(s):
        return pl.ds(pl.multiple_of(128 * s, 128), 128)

    l_ring = Ring(sems, y, yp, ym, lambda s: lbuf.at[p, :, :, column_chunk(s)], lambda s, h: lbuf.at[p, pl.ds(8 * h, 8), :, column_chunk(s)])
    r_ring = Ring(sems, y, yp, ym, lambda s: rj.at[:, :, column_chunk(s)], lambda s, h: rj.at[pl.ds(8 * h, 8), :, column_chunk(s)])
    swaps = {"l": sems.take(4), "w": sems.take(4), "a": sems.take(16), "g": sems.take(1)}

    def swap(kind, slot, ref):
        return sems.copy(ref, ref, swaps[kind] + slot, swaps[kind] + slot, mate)

    def left_swap(n, owner):
        s = (l_ring.me, l_ring.left, l_ring.right, l_ring.far)[n]
        return swap("l", n, lbuf.at[owner, :, :, column_chunk(s)])

    def inv_swap(k, n, owner):
        slot = lax.rem(x + n, 4)
        return swap("a", 4 * k + n, abuf.at[k, pl.ds(k, 4 - k), slot, owner])

    def inv_send(*slots):
        for n in slots:
            for k in range(4):
                inv_swap(k, n, p).start()

    def weight_swap(owner):
        return swap("g", 0, weight.at[owner])

    def w_swap(k, owner):
        return swap("w", k, wbuf.at[owner, 512 * k:512 * k + 512])

    def compute_s():
        for b in range(4):
            acc = None
            for k in range(b + 1):
                term = jnp.dot(abuf[k, b].reshape(512, 512), rj[4 * k:4 * k + 4].reshape(512, 512), preferred_element_type=F32)
                acc = term if acc is None else acc + term
            sj[b] = acc.astype(BF)

    def compute_w():
        for k in range(4):
            acc = None
            for b in range(k, 4):
                term = dot_tn(abuf[k, b].reshape(512, 512), sj[b])
                acc = term if acc is None else acc + term
            wbuf[p, 512 * k:512 * k + 512] = acc.astype(BF)

    def compute_core(t, n):
        j = p if n == 0 else 1 - p
        k_live = lax.broadcasted_iota(jnp.int32, (512, 512), 1) < rank_ref[4 * row + t]
        l_live = lax.broadcasted_iota(jnp.int32, (512, 512), 0) < rank_ref[2 * col + j]
        acc = dot_tn(wbuf[j], rbuf[t].reshape(2048, 512))
        cores[j, t] = jnp.where(jnp.logical_and(k_live, l_live), acc, 0.0).astype(BF)

    def compute_weight():
        factor = lbuf[p].reshape(2048, 512)
        weight[p] = (dot_tn(factor, factor) * (1.0 / 2048)).astype(BF)

    def compute_gram(t):
        @pl.loop(0, 2)
        def _(j):
            core = cores[j, t]
            half = jnp.dot(weight[j], core, preferred_element_type=F32).astype(BF)
            grams[t, j] = dot_tn(core, half).astype(BF)

    def l_start():
        l_ring.start()
        left_swap(0, p).start()

    def l_finish():
        l_ring.finish()
        for n in range(1, 4):
            left_swap(n, p).start()

    def l_take():
        for n in range(4):
            left_swap(n, 1 - p).wait_recv()

    def inv_take():
        for k in range(4):
            for n in range(4):
                inv_swap(k, n, 1 - p).wait_recv()

    def w_send():
        for k in range(4):
            w_swap(k, p).start()

    def w_take():
        for k in range(4):
            w_swap(k, 1 - p).wait_recv()

    def drain_early():
        for which in range(2):
            drain_pieces(which)
        for rings in inv:
            for ring in rings:
                ring.drain()
        for t in range(4):
            right[t][0].drain()
            right[t][1].drain()
        r_ring.drain()
        for k in range(4):
            for n in range(4):
                inv_swap(k, n, p).wait_send()
            w_swap(k, p).wait_send()

    def drain_left():
        weight_swap(p).wait_send()
        l_ring.drain()
        for k in range(4):
            left_swap(k, p).wait_send()

    for k in range(4):
        own_inv[k].wait()
    own_right.wait()
    inv_first()
    send_pieces(0)
    send_pieces(1)
    start(0, range(4))
    inv_first_forward()
    forward(0, range(4))
    inv_turn()
    inv_send(0)
    start(1, range(4))
    take_pieces(0)
    r_ring.start()
    turn(0, (0,))
    forward(1, range(4))
    turn(0, (1,))
    r_ring.forward()
    take_pieces(1)
    l_start()
    inv_second_forward()
    inv_send(1, 3)
    forward(2, (0,))
    turn(0, (2,))
    turn(1, (0,))
    forward(2, (1,))
    turn(0, (3,))
    inv_second_finish()
    inv_send(2)
    turn(1, (1,))
    r_ring.finish()
    inv_take()
    compute_s()
    forward(3, (0,))
    turn(1, (2,))
    compute_w()
    w_send()
    forward(2, (2,))
    turn(1, (3,))
    l_ring.forward()
    finish(2, (0,))
    finish(3, (0,))
    forward(3, (1,))
    compute_core(0, 0)
    w_take()
    compute_core(0, 1)
    l_finish()
    compute_weight()
    forward(2, (3,))
    forward(3, (2,))
    finish(2, (1,))
    finish(3, (1,))
    compute_core(1, 0)
    forward(3, (3,))
    weight_swap(p).start()
    compute_core(1, 1)
    finish(2, (2,))
    finish(3, (2,))
    compute_core(2, 0)
    compute_core(2, 1)
    weight_swap(1 - p).wait_recv()
    compute_gram(0)
    compute_gram(1)
    drain_early()
    compute_gram(2)
    finish(2, (3,))
    finish(3, (3,))
    l_take()
    drain_left()
    compute_core(3, 0)
    compute_core(3, 1)
    compute_gram(3)
    for t in range(4):
        right[t][2].drain()
        right[t][3].drain()


def gather(pan_left, pan_right, inverse, rank_list):
    return pl.pallas_call(
        gather_kernel,
        out_shape=(
            pltpu.VMEM((2, 4, 512, 512), BF), pltpu.VMEM((2, 16, 128, 512), BF), pltpu.VMEM((4, 2, 512, 512), BF),
        ),
        in_specs=[pl.BlockSpec(memory_space=pltpu.HBM)] * 3 + [pl.BlockSpec(memory_space=pltpu.SMEM)],
        out_specs=[pl.BlockSpec(memory_space=pltpu.VMEM)] * 3,
        scratch_shapes=[
            pltpu.VMEM((4, 4, 4, 128, 512), BF),
            pltpu.VMEM((4, 4, 4, 2, 64, 512), BF),
            pltpu.VMEM((2, 2048, 512), BF),
            pltpu.VMEM((16, 128, 512), BF),
            pltpu.VMEM((4, 512, 512), BF),
            pltpu.VMEM((2, 512, 512), BF),
            pltpu.SemaphoreType.DMA((161,)),
            pltpu.SemaphoreType.DMA((161,)),
            pltpu.SemaphoreType.DMA((7,)),
        ],
        compiler_params=pltpu.CompilerParams(collective_id=0, has_side_effects=True, vmem_limit_bytes=54329344),
        name="gather",
    )(pan_left, pan_right, inverse.reshape(2, 64, 2048), rank_list)


def update_kernel(core_ref, left_ref, gram_in, update_ref, gram_ref):
    j, i = pl.program_id(0), pl.program_id(1)
    update_ref[0, 0] = jnp.dot(left_ref[j].reshape(2048, 512), core_ref[j, i], preferred_element_type=F32).astype(BF)
    gram_ref[0, 0] = gram_in[i, j]


def local(pan_left, pan_right, inverse, rank_list):
    core, left, gram = gather(pan_left, pan_right, inverse, rank_list)
    return pl.pallas_call(
        update_kernel,
        grid=(2, 4),
        out_shape=(jax.ShapeDtypeStruct((4, 2, 2048, 512), BF), jax.ShapeDtypeStruct((4, 2, 512, 512), BF)),
        in_specs=[pl.BlockSpec(memory_space=pltpu.VMEM)] * 3,
        out_specs=(
            pl.BlockSpec((1, 1, 2048, 512), lambda j, i: (i, j, 0, 0)),
            pl.BlockSpec((1, 1, 512, 512), lambda j, i: (i, j, 0, 0)),
        ),
        compiler_params=pltpu.CompilerParams(vmem_limit_bytes=24 << 20),
        name="update",
    )(core, left, gram)


def solution(mesh):
    in_specs = (P("row", "col", None), P("row", "col", None), P("col", None), P())
    out_specs = (P("row", "col", None, None), P("row", "col", None, None))
    return jax.shard_map(local, mesh=mesh, in_specs=in_specs, out_specs=out_specs, check_vma=False)
```
